32 devices in a mesh: seq: 4 (over x, core), fsdp: 8 (over z, y).
Axes of the slice: x: 2, y: 2, z: 4, core: 2. Of those that a mesh axis runs over, the one named last changes fastest.
Arguments:
- tokens: bfloat16 [8, 1024, 1536], P('fsdp', 'seq'), may hold values from -6 to 6
- cotangent: bfloat16 [8, 1024, 1536], P('fsdp', 'seq'), may hold values from -6 to 6
- doc_lengths: int32 [8, 8], P('fsdp'), may hold values from 1 to 512, 1024 in all within a row
- w_qkv: float32 [1536, 2048], P(('seq', 'fsdp')), may hold values from -0.15625 to 0.15625
- w_out: float32 [1536, 1536], P(('seq', 'fsdp')), may hold values from -1.5 to 1.5
- w_gate_up: float32 [1536, 17920], P(('seq', 'fsdp')), may hold values from -0.15625 to 0.15625
- w_down: float32 [8960, 1536], P(('seq', 'fsdp')), may hold values from -0.0625 to 0.0625
- small_params: float32 [5120], P(('seq', 'fsdp')), may hold values from -2 to 4.5
- first_qkv: float32 [1536, 2048], P(('seq', 'fsdp')), may hold values from -0.66 to 0.66
- first_out: float32 [1536, 1536], P(('seq', 'fsdp')), may hold values from -0.66 to 0.66
- first_gate_up: float32 [1536, 17920], P(('seq', 'fsdp')), may hold values from -0.66 to 0.66
- first_down: float32 [8960, 1536], P(('seq', 'fsdp')), may hold values from -0.66 to 0.66
- first_small: float32 [5120], P(('seq', 'fsdp')), may hold values from -0.66 to 0.66
- second_qkv: float32 [1536, 2048], P(('seq', 'fsdp')), may hold values from 0.001 to 0.004
- second_out: float32 [1536, 1536], P(('seq', 'fsdp')), may hold values from 0.001 to 0.004
- second_gate_up: float32 [1536, 17920], P(('seq', 'fsdp')), may hold values from 0.001 to 0.004
- second_down: float32 [8960, 1536], P(('seq', 'fsdp')), may hold values from 0.001 to 0.004
- second_small: float32 [5120], P(('seq', 'fsdp')), may hold values from 0.001 to 0.004
Outputs:
- block_out: bfloat16 [8, 1024, 1536], P('fsdp', 'seq')
- tokens_grad: bfloat16 [8, 1024, 1536], P('fsdp', 'seq')
- grad_norm: float32 [], replicated
- matrix_norms: float32 [2, 12], replicated
- updated_qkv: float32 [1536, 2048], P(('seq', 'fsdp'))
- updated_out: float32 [1536, 1536], P(('seq', 'fsdp'))
- updated_gate_up: float32 [1536, 17920], P(('seq', 'fsdp'))
- updated_down: float32 [8960, 1536], P(('seq', 'fsdp'))
- updated_small: float32 [5120], P(('seq', 'fsdp'))
- mean_qkv: float32 [1536, 2048], P(('seq', 'fsdp'))
- mean_out: float32 [1536, 1536], P(('seq', 'fsdp'))
- mean_gate_up: float32 [1536, 17920], P(('seq', 'fsdp'))
- mean_down: float32 [8960, 1536], P(('seq', 'fsdp'))
- mean_small: float32 [5120], P(('seq', 'fsdp'))
- square_qkv: float32 [1536, 2048], P(('seq', 'fsdp'))
- square_out: float32 [1536, 1536], P(('seq', 'fsdp'))
- square_gate_up: float32 [1536, 17920], P(('seq', 'fsdp'))
- square_down: float32 [8960, 1536], P(('seq', 'fsdp'))
- square_small: float32 [5120], P(('seq', 'fsdp'))
The draws below stay inside these ranges and needn't reach their ends.
Inputs may be any that keep to these rules, and one draw needn't show every extreme that they name: `doc_lengths`: the lengths of a row sum to 1024.
All inputs are finite; a program needn't handle non-finite values.
Results may differ from the reference program's by a relative error of at most 0.015.
The reference program's roundings to bfloat16 on the way count: a program that leaves them out, or rounds other values in their place, can miss the bound.
Values may be sent and summed in bfloat16 or wider, within the bound.
A program may use at most 512 MiB of HBM per device.

```python
import math
import jax
import jax.numpy as jnp
import numpy as np
from jax import lax

D = 1536
HEADS = 12
KV_HEADS = 2
HEAD_DIM = 128
FF = 8960
DOCS = 8
QKV = 2048
NPARAMS = 46797824
LEN = 1024
ROWS = 8
DOC_MOST = 512


def draw_small_params(key, part):
    key_bias = jax.random.fold_in(key, 11)
    key_gain = jax.random.fold_in(key, 12)
    bias = jnp.clip(0.5 * jax.random.normal(key_bias, (QKV,), jnp.float32), -2.0, 2.0)
    place = (jnp.arange(2 * D) % D).astype(jnp.float32) / D
    rough = jax.random.uniform(key_gain, (2 * D,), jnp.float32, 0.8, 1.25)
    gains = 0.55 * jnp.exp(place * math.log(3.0)) * rough
    return jnp.concatenate([bias, gains])


def block_scale(own_key, shape, split, low, high):
    level, own = 1.0, jax.random.fold_in(own_key, 6)
    for axis_at, blocks in split:
        heights = jnp.exp(jax.random.uniform(jax.random.fold_in(own, axis_at), (blocks,), jnp.float32, low / len(split), high / len(split)))
        level = level * jnp.repeat(heights, shape[axis_at] // blocks).reshape([-1 if axis == axis_at else 1 for axis in range(len(shape))])
    return level


def profile(number_of, total, reach, slope):
    loads = [(1 << 20) // math.isqrt(grade ** slope) + 1 for grade in range(2, number_of + 1)]
    spare, holding = total - reach - (number_of - 1), [1] * (number_of - 1)
    while spare > 0:
        free = [i for i in range(number_of - 1) if holding[i] < reach]
        mass, budget = sum([loads[i] for i in free]), spare
        for i in free:
            more = min(reach - holding[i], max(1, budget * loads[i] // mass), spare)
            holding[i] = holding[i] + more
            spare = spare - more
    return np.array([reach] + holding)


def uneven(own_key, count, total, most, slope):
    if count == 2:
        one = jax.random.randint(own_key, (), max(1, total - most), min(most, total - 1) + 1)
        return jnp.stack([one, total - one])
    sizes = jnp.asarray(profile(count, total, most, slope), jnp.int32)
    couples = (count - 1) // 2
    source_of, taker = sizes[1:1 + 2 * couples:2], sizes[2:2 + 2 * couples:2]
    slack = jnp.minimum(source_of - 1, most - taker)
    shifted = jax.random.randint(jax.random.fold_in(own_key, 1), (couples,), 0, 1 << 20) % (slack + 1)
    sizes = sizes.at[1:1 + 2 * couples:2].set(source_of - shifted).at[2:2 + 2 * couples:2].set(taker + shifted)
    return sizes[jax.random.permutation(jax.random.fold_in(own_key, 2), count)]


def centred(key, shape, deviation, limit, pieces=(), kind=jnp.bfloat16):
    values = jax.random.normal(key, shape, jnp.float32) * deviation
    if len(pieces) > 0:
        values = block_scale(key, shape, pieces, -0.22, 0.18) * values
    return jnp.clip(values, min=-limit, max=limit).astype(kind)


def setup_inputs(seed: int = 0) -> dict:
    key_list = jax.random.split(jax.random.key(seed), 19)
    return {
        "tokens": centred(key_list[0], (ROWS, LEN, D), 1.0, 6.0, ((0, 8), (1, 4))),
        "cotangent": centred(key_list[1], (ROWS, LEN, D), 1.0, 6.0, ((0, 8), (1, 4))),
        "doc_lengths": jax.vmap(lambda own: uneven(own, DOCS, LEN, DOC_MOST, 1))(jax.random.split(key_list[2], ROWS)).reshape((ROWS, DOCS)).astype(jnp.int32),
        "w_qkv": centred(key_list[3], (D, QKV), D ** -0.5, 0.15625, ((0, 32),), jnp.float32),
        "w_out": centred(key_list[4], (HEADS * HEAD_DIM, D), 16 ** -0.5, 1.5, ((0, 32),), jnp.float32),
        "w_gate_up": centred(key_list[5], (D, 2 * FF), D ** -0.5, 0.15625, ((0, 32),), jnp.float32),
        "w_down": centred(key_list[6], (FF, D), FF ** -0.5, 0.0625, ((0, 32),), jnp.float32),
        "small_params": draw_small_params(jax.random.fold_in(key_list[18], 71), 0),
        "first_qkv": centred(key_list[8], (D, QKV), 0.11, 0.66, ((0, 32),), jnp.float32),
        "first_out": centred(key_list[9], (HEADS * HEAD_DIM, D), 0.11, 0.66, ((0, 32),), jnp.float32),
        "first_gate_up": centred(key_list[10], (D, 2 * FF), 0.11, 0.66, ((0, 32),), jnp.float32),
        "first_down": centred(key_list[11], (FF, D), 0.11, 0.66, ((0, 32),), jnp.float32),
        "first_small": centred(key_list[12], (QKV + 2 * D,), 0.11, 0.66, ((0, 32),), jnp.float32),
        "second_qkv": jnp.clip(jnp.exp(math.log(0.004) - 1.3862944 * jax.random.uniform(key_list[13], (D, QKV), jnp.float32) ** block_scale(key_list[13], (D, QKV), ((0, 32),), -0.2, 0.2)), 0.001, 0.004),
        "second_out": jnp.clip(jnp.exp(math.log(0.004) - 1.3862944 * jax.random.uniform(key_list[14], (HEADS * HEAD_DIM, D), jnp.float32) ** block_scale(key_list[14], (HEADS * HEAD_DIM, D), ((0, 32),), -0.2, 0.2)), 0.001, 0.004),
        "second_gate_up": jnp.clip(jnp.exp(math.log(0.004) - 1.3862944 * jax.random.uniform(key_list[15], (D, 2 * FF), jnp.float32) ** block_scale(key_list[15], (D, 2 * FF), ((0, 32),), -0.2, 0.2)), 0.001, 0.004),
        "second_down": jnp.clip(jnp.exp(math.log(0.004) - 1.3862944 * jax.random.uniform(key_list[16], (FF, D), jnp.float32) ** block_scale(key_list[16], (FF, D), ((0, 32),), -0.2, 0.2)), 0.001, 0.004),
        "second_small": jnp.clip(jnp.exp(math.log(0.004) - 1.3862944 * jax.random.uniform(key_list[17], (QKV + 2 * D,), jnp.float32) ** block_scale(key_list[17], (QKV + 2 * D,), ((0, 32),), -0.2, 0.2)), 0.001, 0.004),
    }


@jax.custom_vjp
def low(v):
    return lax.optimization_barrier(v.astype(jnp.bfloat16)).astype(jnp.float32)

@jax.custom_vjp
def low_back(v):
    return v

def low_keep(v):
    return (low(v), None)

def low_pass(kept, grad):
    return (grad,)

def back_keep(v):
    return (v, None)

def back_low(kept, grad):
    return (low(grad),)
low.defvjp(low_keep, low_pass)
low_back.defvjp(back_keep, back_low)
eps_norm = 1e-06
rope_base = 10000.0
beta_one = 0.9
beta_two = 0.999
lamb_eps = 1e-06
decay_rate = 0.01
learn_rate = 1.0
step_count = 10
trust_eps = 1e-06
masked_score = -1e+30
piece_count = 12

def matmul(left, right):
    return jnp.dot(left, right, precision=lax.Precision.HIGHEST)

def normed(values, gain):
    factor = lax.rsqrt(lax.optimization_barrier(jnp.mean(values * values, axis=-1, keepdims=True)) + eps_norm)
    return values * factor * gain

def rope_tables(positions, width):
    half = width // 2
    freq = jnp.exp(jnp.arange(half).astype(jnp.float32) * (-2.0 * math.log(rope_base) / width))
    angle = positions.astype(jnp.float32)[:, None] * freq[None, :]
    angle = jnp.concatenate([angle, angle], axis=-1)
    return (jnp.cos(angle)[:, None, :], jnp.sin(angle)[:, None, :])

def rope_turn(values, cosine, sine):
    half = values.shape[-1] // 2
    turned = jnp.concatenate([-values[..., half:], values[..., :half]], axis=-1)
    return values * cosine + turned * sine

def doc_starts(lengths, places):
    ends = jnp.cumsum(lengths)
    return lax.optimization_barrier(jnp.sum(jnp.where(ends[None, :] <= places[:, None], lengths[None, :], 0), axis=1)).astype(jnp.int32)

def layer(values, qkv_master, out_master, gate_up_master, down_master, small_master, places, starts):
    heads_width = HEADS * HEAD_DIM
    kv_width = KV_HEADS * HEAD_DIM
    group = HEADS // KV_HEADS
    score_scale = 1.0 / math.sqrt(HEAD_DIM)
    qkv_w = low(qkv_master)
    out_w = low(out_master)
    gate_up_w = low(gate_up_master)
    down_w = low(down_master)
    small_w = low(small_master)
    bias = small_w[:QKV]
    gain_one = small_w[QKV:QKV + D]
    gain_two = small_w[QKV + D:]
    normed_one = low(normed(values, gain_one))
    projected = low_back(matmul(normed_one, qkv_w) + bias)
    query = projected[:, :heads_width].reshape(LEN, HEADS, HEAD_DIM)
    keys = projected[:, heads_width:heads_width + kv_width].reshape(LEN, KV_HEADS, HEAD_DIM)
    value_heads = projected[:, heads_width + kv_width:].reshape(LEN, KV_HEADS, HEAD_DIM)
    cosine, sine = rope_tables(places - starts, HEAD_DIM)
    query = low(rope_turn(query, cosine, sine))
    keys = low(rope_turn(keys, cosine, sine))
    value_heads = low(value_heads)
    allowed = (places[None, :] <= places[:, None]) & (places[None, :] >= starts[:, None])

    def attend_block(parts):
        block_query, block_keys, block_values = parts
        scores = jnp.einsum('tgd,kd->tgk', block_query, block_keys, precision=lax.Precision.HIGHEST) * score_scale
        scores = low_back(jnp.where(allowed[:, None, :], scores, masked_score))
        probs = low(jax.nn.softmax(scores, axis=-1))
        return jnp.einsum('tgk,kd->tgd', probs, block_values, precision=lax.Precision.HIGHEST)
    grouped = query.reshape(LEN, KV_HEADS, group, HEAD_DIM).transpose(1, 0, 2, 3)
    mixed = lax.map(jax.checkpoint(attend_block), (grouped, keys.transpose(1, 0, 2), value_heads.transpose(1, 0, 2)))
    mixed = mixed.transpose(1, 0, 2, 3).reshape(LEN, heads_width)
    mixed_low = low(low_back(mixed))
    middle = values + low_back(matmul(mixed_low, out_w))
    normed_two = low(normed(middle, gain_two))
    gate_up = low_back(matmul(normed_two, gate_up_w))
    hidden = low(jax.nn.silu(gate_up[:, :FF]) * gate_up[:, FF:])
    return middle + low_back(matmul(hidden, down_w))

def part_labels(count, bounds, first):
    index = jnp.arange(count).astype(jnp.int32)
    label = jnp.full((count,), first, jnp.int32)
    for bound in bounds:
        label = label + (index >= bound).astype(jnp.int32)
    return label

def piece_sums(values, labels):
    onehot = labels[:, None] == jnp.arange(piece_count).astype(jnp.int32)[None, :]
    return lax.optimization_barrier(jnp.sum(jnp.where(onehot, values[:, None], jnp.zeros_like(values)[:, None]), axis=0))

def column_squares(values):
    if values.ndim == 1:
        return values * values
    return lax.optimization_barrier(jnp.sum(values * values, axis=0))

def spread_trust(trust, labels):
    onehot = labels[:, None] == jnp.arange(piece_count).astype(jnp.int32)[None, :]
    return lax.optimization_barrier(jnp.sum(jnp.where(onehot, trust[None, :], jnp.zeros_like(trust)[None, :]), axis=1))

def reference(tokens, cotangent, doc_lengths, w_qkv, w_out, w_gate_up, w_down, small_params, first_qkv, first_out, first_gate_up, first_down, first_small, second_qkv, second_out, second_gate_up, second_down, second_small):
    masters = (w_qkv, w_out, w_gate_up, w_down, small_params)
    firsts = (first_qkv, first_out, first_gate_up, first_down, first_small)
    seconds = (second_qkv, second_out, second_gate_up, second_down, second_small)
    places = jnp.arange(LEN).astype(jnp.int32)

    def one_row(carry, items):
        row_tokens, row_cot, row_lengths = items
        starts = doc_starts(row_lengths, places)

        def forward(values, qkv_master, out_master, gate_up_master, down_master, small_master):
            return layer(values, qkv_master, out_master, gate_up_master, down_master, small_master, places, starts)
        row_out, back = jax.vjp(forward, row_tokens.astype(jnp.float32), *masters)
        grads = back(row_cot.astype(jnp.float32))
        carry = tuple((kept + new for kept, new in zip(carry, grads[1:])))
        return (carry, (row_out.astype(jnp.bfloat16), grads[0].astype(jnp.bfloat16)))
    zeros = tuple((jnp.zeros(master.shape, jnp.float32) for master in masters))
    grads, (block_out, tokens_grad) = lax.scan(one_row, zeros, (tokens, cotangent, doc_lengths))
    heads_width = HEADS * HEAD_DIM
    kv_width = KV_HEADS * HEAD_DIM
    labels = (part_labels(QKV, [heads_width, heads_width + kv_width], 0), part_labels(D, [], 3), part_labels(2 * FF, [FF], 4), part_labels(D, [], 6), part_labels(QKV + 2 * D, [heads_width, heads_width + kv_width, QKV, QKV + D], 7))
    grad_total = jnp.sum(jnp.stack([jnp.sum(grad * grad) for grad in grads]))
    grad_norm = jnp.sqrt(grad_total)
    factor = jnp.minimum(1.0, math.sqrt(NPARAMS) / grad_norm)
    weight_total = lax.optimization_barrier(jnp.sum(jnp.stack([piece_sums(column_squares(master), label) for master, label in zip(masters, labels)]), axis=0))
    results = []
    for master, grad, first, second in zip(masters, grads, firsts, seconds):
        clipped = grad * factor
        first_new = beta_one * first + (1.0 - beta_one) * clipped
        second_new = beta_two * second + (1.0 - beta_two) * clipped * clipped
        update = first_new / (1.0 - beta_one ** step_count) / (jnp.sqrt(second_new / (1.0 - beta_two ** step_count)) + lamb_eps) + decay_rate * master
        results.append((first_new, second_new, update))
    update_total = lax.optimization_barrier(jnp.sum(jnp.stack([piece_sums(column_squares(item[2]), label) for item, label in zip(results, labels)]), axis=0))
    weight_norm = jnp.sqrt(weight_total)
    update_norm = jnp.sqrt(update_total)
    trust = weight_norm / (update_norm + trust_eps)
    updated = [master - learn_rate * spread_trust(trust, label) * item[2] for master, item, label in zip(masters, results, labels)]
    matrix_norms = jnp.stack([weight_norm, update_norm])
    return (block_out, tokens_grad, grad_norm, matrix_norms, updated[0], updated[1], updated[2], updated[3], updated[4], results[0][0], results[1][0], results[2][0], results[3][0], results[4][0], results[0][1], results[1][1], results[2][1], results[3][1], results[4][1])
```

```python
from functools import partial
import itertools
import math

import jax
import jax.numpy as jnp
from jax import lax
from jax.experimental import pallas as pl
from jax.experimental.pallas import tpu as pltpu
from jax.sharding import Mesh, PartitionSpec as P

D = 1536
HEADS = 12
KV_HEADS = 2
HEAD_DIM = 128
FF = 8960
QKV = 2048
NPARAMS = 46797824


eps_norm = 1e-06
rope_base = 10000.0
beta_one = 0.9
beta_two = 0.999
lamb_eps = 1e-06
decay_rate = 0.01
learn_rate = 1.0
step_count = 10
trust_eps = 1e-06
masked_score = -1e30
piece_count = 12


def normed(values, gain):
    factor = lax.rsqrt(jnp.mean(values * values, axis=-1, keepdims=True) + eps_norm)
    return values * factor * gain


def rope_tables(positions, width):
    half = width // 2
    freq = jnp.exp(jnp.arange(half).astype(jnp.float32) * (-2.0 * math.log(rope_base) / width))
    angle = positions.astype(jnp.float32)[:, None] * freq[None, :]
    angle = jnp.concatenate([angle, angle], axis=-1)
    return (jnp.cos(angle)[:, None, :], jnp.sin(angle)[:, None, :])


def rope_turn(values, cosine, sine):
    half = values.shape[-1] // 2
    turned = jnp.concatenate([-values[..., half:], values[..., :half]], axis=-1)
    return values * cosine + turned * sine


def swish_product(gate, upper):
    return jax.nn.silu(gate) * upper


def doc_starts(lengths, places):
    ends = jnp.cumsum(lengths)
    return jnp.sum(jnp.where(ends[None, :] <= places[:, None], lengths[None, :], 0), axis=1)


def contract_rows(left, right):
    return lax.dot_general(
        left, right, (((0,), (0,)), ((), ())), preferred_element_type=jnp.float32
    )


def contract_cols(left, right):
    return lax.dot_general(
        left, right, (((1,), (1,)), ((), ())), preferred_element_type=jnp.float32
    )


def part_labels(count, bounds, first, offset):
    index = offset + jnp.arange(count)
    label = jnp.full((count,), first, jnp.int32)
    for bound in bounds:
        label = label + (index >= bound).astype(jnp.int32)
    return label


def piece_sums(values, labels):
    onehot = labels[:, None] == jnp.arange(piece_count)[None, :]
    return jnp.sum(jnp.where(onehot, values[:, None], 0.0), axis=0)


def column_squares(values):
    if values.ndim == 1:
        return values * values
    return jnp.sum(values * values, axis=0)


def spread_trust(trust, labels):
    onehot = labels[:, None] == jnp.arange(piece_count)[None, :]
    return jnp.sum(jnp.where(onehot, trust[None, :], 0.0), axis=1)


EVERY = ("x", "core", "z", "y")
KEEPERS = ("x", "core", "y")
LINKED = pl.DeviceIdType.MESH


def place_of(axes):
    index = 0
    for axis in axes:
        index = index * lax.axis_size(axis) + lax.axis_index(axis)
    return index


def partner(axes, offset):
    where, index = {}, 0
    for axis, step in zip(axes, offset):
        size = lax.axis_size(axis)
        at = lax.rem(lax.axis_index(axis) + step, size)
        where[axis] = at
        index = index * size + at
    return where, index


def hello(partners):
    barrier = pltpu.get_barrier_semaphore()
    for where in partners:
        pl.semaphore_signal(barrier, inc=1, device_id=where, device_id_type=LINKED)
    pl.semaphore_wait(barrier, len(partners))


def push(source, target, send, recv, where):
    copy = pltpu.make_async_remote_copy(
        src_ref=source,
        dst_ref=target,
        send_sem=send,
        recv_sem=recv,
        device_id=where,
        device_id_type=LINKED,
    )
    copy.start()
    return copy


def every_offset(axes):
    return [o for o in itertools.product(*[range(lax.axis_size(a)) for a in axes]) if any(o)]


def exchange_kernel(axes, offsets, cuts, *refs):
    n = len(cuts)
    sources, targets, (send_sem, recv_sem, own_sem) = refs[:n], refs[n : 2 * n], refs[2 * n :]
    me = place_of(axes)
    partners = [partner(axes, offset) for offset in offsets]
    owns = []
    for a in range(n):
        own = pltpu.make_async_copy(
            sources[a].at[me] if cuts[a] else sources[a], targets[a].at[me], own_sem.at[a]
        )
        own.start()
        owns.append(own)
    hello([where for where, _ in partners])
    copies = []
    for k, (where, index) in enumerate(partners):
        for a in range(n):
            copies.append(
                push(
                    sources[a].at[index] if cuts[a] else sources[a],
                    targets[a].at[me],
                    send_sem.at[a, k],
                    recv_sem.at[a, k],
                    where,
                )
            )
    for copy in owns + copies:
        copy.wait()


def exchange(values, axes, cuts, number, space=pl.ANY):
    offsets = every_offset(axes)
    count, n = len(offsets), len(values)
    return pl.pallas_call(
        partial(exchange_kernel, axes, offsets, cuts),
        out_shape=[
            jax.ShapeDtypeStruct(v.shape if cut else (count + 1,) + v.shape, v.dtype)
            for v, cut in zip(values, cuts)
        ],
        in_specs=[pl.BlockSpec(memory_space=space)] * n,
        out_specs=[pl.BlockSpec(memory_space=space)] * n,
        scratch_shapes=[
            pltpu.SemaphoreType.DMA((n, count)),
            pltpu.SemaphoreType.DMA((n, count)),
            pltpu.SemaphoreType.DMA((n,)),
        ],
        compiler_params=pltpu.CompilerParams(collective_id=number, has_side_effects=True),
    )(*values)


def spread_kernel(n, m, *refs):
    sources, rest = refs[: n + m], refs[n + m :]
    targets, (send_sem, recv_sem, cut_send, cut_recv, own_sem) = rest[: n + m], rest[n + m :]
    deep = lax.axis_size("z")
    x, core, z, y = [lax.axis_index(a) for a in EVERY]
    me = place_of(EVERY)
    offsets = every_offset(EVERY)
    partners = [partner(EVERY, offset) for offset in offsets]
    owns = []
    for a in range(n + m):
        own = pltpu.make_async_copy(
            sources[a] if a < n else sources[a].at[me],
            targets[a].at[x, core, z, y] if a < n else targets[a].at[me],
            own_sem.at[a],
        )
        own.start()
        owns.append(own)
    hello([where for where, _ in partners])

    def owner(dx, dc, dz, dy):
        return (lax.rem(x + dx, 2), lax.rem(core + dc, 2), lax.rem(z + dz, deep), lax.rem(y + dy, 2))

    def slot(dx, dc, dz, dy):
        return ((dx * 2 + dc) * deep + dz) * 2 + dy

    pending = []

    def forward(block, axis, step):
        there = dict(zip(("x", "core", "z", "y"), block))
        size = lax.axis_size(axis)
        there[axis] = (there[axis] - step) % size
        k = slot(*[there[a] for a in EVERY])
        where = {axis: lax.rem(lax.axis_index(axis) + step, size)}
        at = owner(*block)
        for a in range(n):
            held = sources[a] if not any(block) else targets[a].at[at]
            pending.append(push(held, targets[a].at[at], send_sem.at[a, k], recv_sem.at[a, k], where))

    def arrived(block):
        k = slot(*block)
        at = owner(*block)
        for a in range(n):
            pltpu.make_async_remote_copy(
                src_ref=sources[a],
                dst_ref=targets[a].at[at],
                send_sem=send_sem.at[a, k],
                recv_sem=recv_sem.at[a, k],
                device_id={"core": lax.rem(core + 1, 2)},
                device_id_type=LINKED,
            ).wait_recv()

    own_block = (0, 0, 0, 0)
    forward(own_block, "x", 1)
    forward(own_block, "y", 1)
    for step in range(1, deep):
        forward(own_block, "z", step)
    forward(own_block, "core", 1)
    cut_copies = []
    for k, (where, index) in enumerate(partners):
        for a in range(m):
            cut_copies.append(
                push(
                    sources[n + a].at[index],
                    targets[n + a].at[me],
                    cut_send.at[a, k],
                    cut_recv.at[a, k],
                    where,
                )
            )
    for dz in range(deep):
        if dz > 0:
            arrived((0, 0, dz, 0))
            forward((0, 0, dz, 0), "x", 1)
            forward((0, 0, dz, 0), "y", 1)
            forward((0, 0, dz, 0), "core", 1)
        for block, axis, parity in (((1, 0, dz, 0), "y", 1), ((0, 0, dz, 1), "x", 0)):
            arrived(block)
            if dz % 2 == parity:
                forward(block, axis, 1)
            forward(block, "core", 1)
    for dz in range(deep):
        arrived((1, 0, dz, 1))
        forward((1, 0, dz, 1), "core", 1)
    for dx in range(2):
        for dz in range(deep):
            for dy in range(2):
                arrived((dx, 1, dz, dy))
    for copy in pending:
        copy.wait_send()
    for copy in owns + cut_copies:
        copy.wait()


def spread(values, cut_values, number):
    n, m = len(values), len(cut_values)
    sizes = tuple(lax.axis_size(a) for a in EVERY)
    count = math.prod(sizes)
    if sizes[:2] != (2, 2) or sizes[3] != 2:
        return [lax.all_gather(v, EVERY, axis=0, tiled=True) for v in values] + list(
            exchange(cut_values, EVERY, [True] * m, number)
        )
    outs = pl.pallas_call(
        partial(spread_kernel, n, m),
        out_shape=[jax.ShapeDtypeStruct(sizes + v.shape, v.dtype) for v in values]
        + [jax.ShapeDtypeStruct(v.shape, v.dtype) for v in cut_values],
        in_specs=[pl.BlockSpec(memory_space=pl.ANY)] * (n + m),
        out_specs=[pl.BlockSpec(memory_space=pl.ANY)] * (n + m),
        scratch_shapes=[
            pltpu.SemaphoreType.DMA((n, count)),
            pltpu.SemaphoreType.DMA((n, count)),
            pltpu.SemaphoreType.DMA((m, count)),
            pltpu.SemaphoreType.DMA((m, count)),
            pltpu.SemaphoreType.DMA((n + m,)),
        ],
        compiler_params=pltpu.CompilerParams(collective_id=number, has_side_effects=True),
    )(*values, *cut_values)
    return [o.reshape((-1,) + v.shape[1:]) for o, v in zip(outs, values)] + list(outs[n:])


def add_blocks(count, first, second, store):
    def step(i, carry):
        store(i, (first(i).astype(jnp.float32) + second(i).astype(jnp.float32)).astype(jnp.bfloat16))
        return carry

    lax.fori_loop(0, count, step, 0)


def collect_kernel(pieces, width, *refs):
    n = max(a for a, _ in pieces) + 1
    sources, targets, scratch = refs[:n], refs[n : 2 * n], refs[2 * n :]
    r1, a1, r2, a2, r3, a3, r4, send_sem, recv_sem = scratch
    x, core, z, y = [lax.axis_index(a) for a in EVERY]
    deep = lax.axis_size("z")
    half = deep // 2
    other = {a: {a: lax.rem(lax.axis_index(a) + 1, 2)} for a in ("x", "core", "y")}
    zs = [{"z": lax.rem(z + k, deep)} for k in range(1, deep)]
    hello([other["core"], other["x"], other["y"]] + zs)
    total = len(pieces)
    going = [{} for _ in pieces]

    def window(p):
        a, k = pieces[p]
        return sources[a], pl.ds(k * width, width)

    def go(p, name, s, source, target, where):
        going[p][name] = push(source, target, send_sem.at[p, s], recv_sem.at[p, s], where)

    def stage(p, s):
        source, cols = window(p)
        if s == 1:
            go(p, "c", 0, source.at[:, 1 - core, :, :, :, cols], r1.at[p], other["core"])
        if s == 2:
            going[p]["c"].wait()
            for i in range(2):
                for k in range(deep):
                    def put(t, v, i=i, k=k):
                        a1[p, i, k, t] = v
                    add_blocks(
                        2,
                        lambda t, i=i, k=k: source[i, core, k, t, :, cols],
                        lambda t, i=i, k=k: r1[p, i, k, t],
                        put,
                    )
            go(p, "x", 1, a1.at[p, 1 - x, pl.ds(0, half)], r2.at[p, 0], other["x"])
            go(p, "y", 2, a1.at[p, :, pl.ds(half, half), 1 - y], r2.at[p, 1], other["y"])
        if s == 3:
            going[p]["x"].wait()
            going[p]["y"].wait()
            for k in range(half):
                def put_x(t, v, k=k):
                    a2[p, 0, k, t] = v
                add_blocks(
                    2, lambda t, k=k: a1[p, x, k, t], lambda t, k=k: r2[p, 0, k, t], put_x
                )
                def put_y(t, v, k=k):
                    a2[p, 1, t, k] = v
                add_blocks(
                    2, lambda t, k=k: a1[p, t, half + k, y], lambda t, k=k: r2[p, 1, t, k], put_y
                )
            go(p, "y2", 3, a2.at[p, 0, :, 1 - y], r3.at[p, 0], other["y"])
            go(p, "x2", 4, a2.at[p, 1, 1 - x], r3.at[p, 1], other["x"])
        if s == 4:
            going[p]["y2"].wait()
            going[p]["x2"].wait()
            def put_low(t, v):
                a3[p, t] = v
            add_blocks(half, lambda t: a2[p, 0, t, y], lambda t: r3[p, 0, t], put_low)
            def put_high(t, v):
                a3[p, half + t] = v
            add_blocks(half, lambda t: a2[p, 1, x, t], lambda t: r3[p, 1, t], put_high)
            for k in range(1, deep):
                go(p, k, 4 + k, a3.at[p, lax.rem(z + k, deep)], r4.at[p, k - 1], zs[k - 1])
        if s == 5:
            whole = a3[p, z].astype(jnp.float32)
            for k in range(1, deep):
                going[p][k].wait()
                whole = whole + r4[p, k - 1].astype(jnp.float32)
            a, _ = pieces[p]
            targets[a][:, cols] = whole

    for t in range(1, total + 5):
        for s in (5, 4, 3, 2, 1):
            p = t - s
            if 0 <= p < total:
                stage(p, s)


def collect(values, number, width=512):
    sizes = tuple(lax.axis_size(a) for a in EVERY)
    if sizes[:2] != (2, 2) or sizes[3] != 2 or sizes[2] % 2:
        return [
            lax.psum_scatter(v, EVERY, scatter_dimension=0, tiled=True).astype(jnp.float32)
            for v in values
        ]
    rows = values[0].shape[0] // math.prod(sizes)
    deep = sizes[2]
    pieces = [(a, k) for a, v in enumerate(values) for k in range(v.shape[1] // width)]
    total = len(pieces)
    block = (rows, width)
    return pl.pallas_call(
        partial(collect_kernel, pieces, width),
        out_shape=[jax.ShapeDtypeStruct((rows, v.shape[1]), jnp.float32) for v in values],
        in_specs=[pl.BlockSpec(memory_space=pltpu.VMEM)] * len(values),
        out_specs=[pl.BlockSpec(memory_space=pltpu.VMEM)] * len(values),
        scratch_shapes=[
            pltpu.VMEM((total, 2, deep, 2) + block, jnp.bfloat16),
            pltpu.VMEM((total, 2, deep, 2) + block, jnp.bfloat16),
            pltpu.VMEM((total, 2, deep // 2, 2) + block, jnp.bfloat16)
            if deep == 4
            else pltpu.VMEM((total, 2, deep // 2, 2) + block, jnp.bfloat16),
            pltpu.VMEM((total, 2, deep // 2, 2) + block, jnp.bfloat16),
            pltpu.VMEM((total, 2, deep // 2) + block, jnp.bfloat16),
            pltpu.VMEM((total, deep) + block, jnp.bfloat16),
            pltpu.VMEM((total, deep - 1) + block, jnp.bfloat16),
            pltpu.SemaphoreType.DMA((total, 4 + deep)),
            pltpu.SemaphoreType.DMA((total, 4 + deep)),
        ],
        compiler_params=pltpu.CompilerParams(
            collective_id=number, has_side_effects=True, vmem_limit_bytes=56 * 2**20
        ),
    )(*[v.reshape(sizes + (rows, v.shape[1])) for v in values])


def as_tiles(values):
    width = -(-values.shape[-1] // 1024) * 1024
    padded = jnp.pad(values, [(0, 0)] * (values.ndim - 1) + [(0, width - values.shape[-1])])
    return padded.reshape(values.shape[:-1] + (width // 128, 128))


def z_turn(values, step):
    size = lax.axis_size("z")
    return lax.ppermute(values, "z", [(i, (i + step) % size) for i in range(size)])


def z_ring(values):
    blocks = [values]
    for _ in range(lax.axis_size("z") - 1):
        blocks.append(z_turn(blocks[-1], 1))
    return jnp.concatenate(blocks, axis=0)


def z_return(values):
    size = lax.axis_size("z")
    blocks = jnp.split(values, size, axis=0)
    parts = [blocks[0]] + [z_turn(blocks[k], -k) for k in range(1, size)]
    return sum(part.astype(jnp.float32) for part in parts)


def tiny_gather(values, number):
    every = exchange([as_tiles(values)], EVERY, [False], number, pltpu.VMEM)[0]
    return every.reshape(every.shape[0], -1)[:, : values.shape[0]]


def shards(
    tokens,
    cotangent,
    doc_lengths,
    w_qkv,
    w_out,
    w_gate_up,
    w_down,
    small_params,
    first_qkv,
    first_out,
    first_gate_up,
    first_down,
    first_small,
    second_qkv,
    second_out,
    second_gate_up,
    second_down,
    second_small,
):
    heads_width = HEADS * HEAD_DIM
    kv_width = KV_HEADS * HEAD_DIM
    group = HEADS // KV_HEADS
    score_scale = 1.0 / math.sqrt(HEAD_DIM)
    devices = math.prod(lax.axis_size(axis) for axis in EVERY)
    units = FF // devices
    rows_d = D // devices
    wide = -(-2 * units // 128) * 128
    small_wide = tiny_gather(
        small_params.astype(jnp.bfloat16).astype(jnp.float32), 0
    ).reshape(-1)
    cut = w_gate_up.astype(jnp.bfloat16).reshape(rows_d, 2, devices, units).transpose(2, 0, 1, 3)
    cut = jnp.pad(cut.reshape(devices, rows_d, 2 * units), ((0, 0), (0, 0), (0, wide - 2 * units)))
    qkv_full, out_full, traded = spread(
        [w_qkv.astype(jnp.bfloat16), w_out.astype(jnp.bfloat16)], [cut], 1
    )
    own_gate_up = traded.reshape(D, wide)[:, : 2 * units].T
    own_units = jnp.concatenate([own_gate_up, w_down.astype(jnp.bfloat16)], axis=0)
    unit_rows = lax.all_gather(own_units, KEEPERS, axis=0)
    gate_full = unit_rows[:, :units].reshape(-1, D)
    up_full = unit_rows[:, units : 2 * units].reshape(-1, D)
    down_full = unit_rows[:, 2 * units :].reshape(-1, D)
    cot_low = cotangent[0]
    cot_group = z_ring(cot_low)
    bias = small_wide[:QKV]
    gain_one = small_wide[QKV : QKV + D]
    gain_two = small_wide[QKV + D :]
    inputs = tokens[0].astype(jnp.float32)
    rows = inputs.shape[0]
    length = rows * (lax.axis_size("x") * lax.axis_size("core"))
    places = place_of(("x", "core")) * rows + jnp.arange(rows)
    key_places = jnp.arange(length)
    starts = doc_starts(doc_lengths[0], places)
    allowed = (key_places[None, :] <= places[:, None]) & (key_places[None, :] >= starts[:, None])
    cosine, sine = rope_tables(places - starts, HEAD_DIM)
    normed_one = normed(inputs, gain_one).astype(jnp.bfloat16)
    projected = jnp.dot(normed_one, qkv_full, preferred_element_type=jnp.float32) + bias
    query_raw = projected[:, :heads_width].reshape(rows, HEADS, HEAD_DIM)
    key_raw = projected[:, heads_width : heads_width + kv_width].reshape(rows, KV_HEADS, HEAD_DIM)
    value_low = projected[:, heads_width + kv_width :].astype(jnp.bfloat16)
    query_low = rope_turn(query_raw, cosine, sine).astype(jnp.bfloat16)
    key_low = rope_turn(key_raw, cosine, sine).astype(jnp.bfloat16).reshape(rows, kv_width)
    kv_rows = exchange(
        [jnp.concatenate([key_low, value_low], axis=1)], ("x", "core"), [False], 2
    )[0].reshape(length, 2 * kv_width)
    keys_grouped = kv_rows[:, :kv_width].reshape(length, KV_HEADS, HEAD_DIM).transpose(1, 0, 2)
    values_grouped = kv_rows[:, kv_width:].reshape(length, KV_HEADS, HEAD_DIM).transpose(1, 0, 2)
    query_grouped = query_low.reshape(rows, KV_HEADS, group, HEAD_DIM).transpose(1, 0, 2, 3)

    def attend_forward(parts):
        block_query, block_keys, block_values = parts
        scores = (
            jnp.einsum("tgd,kd->tgk", block_query, block_keys, preferred_element_type=jnp.float32)
            * score_scale
        )
        scores = jnp.where(allowed[:, None, :], scores, masked_score)
        highest = jnp.max(scores, axis=-1, keepdims=True)
        weights = jnp.exp(scores - highest)
        totals = jnp.sum(weights, axis=-1, keepdims=True)
        probs_low = (weights / totals).astype(jnp.bfloat16)
        mixed = jnp.einsum(
            "tgk,kd->tgd", probs_low, block_values, preferred_element_type=jnp.float32
        )
        return (mixed, (highest + jnp.log(totals))[..., 0])

    mixed, log_totals = lax.map(attend_forward, (query_grouped, keys_grouped, values_grouped))
    mixed_low = mixed.transpose(1, 0, 2, 3).reshape(rows, heads_width).astype(jnp.bfloat16)
    middle = inputs + jnp.dot(mixed_low, out_full, preferred_element_type=jnp.float32)
    normed_two = normed(middle, gain_two).astype(jnp.bfloat16)
    group_two = z_ring(normed_two)
    gate = contract_cols(group_two, gate_full)
    upper = contract_cols(group_two, up_full)
    hidden, swish_back = jax.vjp(swish_product, gate, upper)
    hidden_low = hidden.astype(jnp.bfloat16)
    d_hidden = contract_cols(cot_group, down_full)
    d_gate, d_upper = swish_back(d_hidden)
    d_gate = d_gate.astype(jnp.bfloat16)
    d_upper = d_upper.astype(jnp.bfloat16)
    d_two_part = jnp.dot(d_gate, gate_full, preferred_element_type=jnp.float32) + jnp.dot(
        d_upper, up_full, preferred_element_type=jnp.float32
    )
    zs = lax.axis_size("z")
    d_normed_two = z_return(d_two_part.astype(jnp.bfloat16))
    mlp_part = jnp.dot(hidden_low, down_full, preferred_element_type=jnp.float32)
    mlp_term = z_return(mlp_part.astype(jnp.bfloat16))
    keepers = devices // zs
    unit_grads = jnp.concatenate(
        [
            contract_rows(a, b).astype(jnp.bfloat16).reshape(keepers, units, D)
            for a, b in ((d_gate, group_two), (d_upper, group_two), (hidden_low, cot_group))
        ],
        axis=1,
    )
    own_grads = lax.psum_scatter(unit_grads, KEEPERS, scatter_dimension=0, tiled=False)
    grad_down = own_grads[2 * units :].astype(jnp.float32)
    back = jnp.pad(own_grads[: 2 * units].T, ((0, 0), (0, wide - 2 * units)))
    back = exchange([back.reshape(devices, rows_d, wide)], EVERY, [True], 6)[0]
    grad_gate_up = (
        back[:, :, : 2 * units]
        .reshape(devices, rows_d, 2, units)
        .transpose(1, 2, 0, 3)
        .reshape(rows_d, 2 * FF)
        .astype(jnp.float32)
    )
    block_out = (middle + mlp_term).astype(jnp.bfloat16)[None]
    unused_two, norm_two_back = jax.vjp(normed, middle, gain_two)
    d_middle_norm, d_gain_two = norm_two_back(d_normed_two)
    d_middle = cot_low.astype(jnp.float32) + d_middle_norm
    d_branch_low = d_middle.astype(jnp.bfloat16)
    grad_out_term = contract_rows(mixed_low, d_branch_low)
    d_mixed_low = contract_cols(d_branch_low, out_full).astype(jnp.bfloat16)
    d_mixed_grouped = d_mixed_low.reshape(rows, KV_HEADS, group, HEAD_DIM).transpose(1, 0, 2, 3)

    def attend_back(parts):
        block_query, block_keys, block_values, block_grad, block_log = parts
        scores = (
            jnp.einsum("tgd,kd->tgk", block_query, block_keys, preferred_element_type=jnp.float32)
            * score_scale
        )
        scores = jnp.where(allowed[:, None, :], scores, masked_score)
        probs = jnp.exp(scores - block_log[..., None])
        probs_low = probs.astype(jnp.bfloat16)
        d_probs = jnp.einsum(
            "tgd,kd->tgk", block_grad, block_values, preferred_element_type=jnp.float32
        )
        d_values = jnp.einsum(
            "tgk,tgd->kd", probs_low, block_grad, preferred_element_type=jnp.float32
        )
        centre = jnp.sum(probs * d_probs, axis=-1, keepdims=True)
        d_scores = (probs * (d_probs - centre)).astype(jnp.bfloat16)
        d_query = (
            jnp.einsum("tgk,kd->tgd", d_scores, block_keys, preferred_element_type=jnp.float32)
            * score_scale
        )
        d_keys = (
            jnp.einsum("tgk,tgd->kd", d_scores, block_query, preferred_element_type=jnp.float32)
            * score_scale
        )
        return (d_query, d_keys, d_values)

    d_query, d_keys, d_values = lax.map(
        attend_back, (query_grouped, keys_grouped, values_grouped, d_mixed_grouped, log_totals)
    )
    d_kv_rows = jnp.concatenate(
        [
            d_keys.transpose(1, 0, 2).reshape(length, kv_width),
            d_values.transpose(1, 0, 2).reshape(length, kv_width),
        ],
        axis=1,
    )
    d_kv_every = exchange(
        [d_kv_rows.astype(jnp.bfloat16).reshape(-1, rows, 2 * kv_width)], ("x", "core"), [True], 3
    )[0]
    d_kv_local = jnp.sum(d_kv_every.astype(jnp.float32), axis=0)
    unused_query, rope_query_back = jax.vjp(partial(rope_turn, cosine=cosine, sine=sine), query_raw)
    unused_key, rope_key_back = jax.vjp(partial(rope_turn, cosine=cosine, sine=sine), key_raw)
    (d_query_raw,) = rope_query_back(d_query.transpose(1, 0, 2, 3).reshape(rows, HEADS, HEAD_DIM))
    (d_key_raw,) = rope_key_back(d_kv_local[:, :kv_width].reshape(rows, KV_HEADS, HEAD_DIM))
    d_projected = jnp.concatenate(
        [
            d_query_raw.reshape(rows, heads_width),
            d_key_raw.reshape(rows, kv_width),
            d_kv_local[:, kv_width:],
        ],
        axis=1,
    ).astype(jnp.bfloat16)
    d_bias = jnp.sum(d_projected.astype(jnp.float32), axis=0)
    grad_qkv_term = contract_rows(normed_one, d_projected)
    d_normed_one = contract_cols(d_projected, qkv_full)
    unused_one, norm_one_back = jax.vjp(normed, inputs, gain_one)
    d_inputs, d_gain_one = norm_one_back(d_normed_one)
    tokens_grad = (d_middle + d_inputs).astype(jnp.bfloat16)[None]
    grad_out, grad_qkv = collect(
        [grad_out_term.astype(jnp.bfloat16), grad_qkv_term.astype(jnp.bfloat16)], 4
    )
    small_terms = jnp.concatenate([d_bias, d_gain_one, d_gain_two]).reshape(devices, -1)
    small_every = exchange([as_tiles(small_terms)], EVERY, [True], 5, pltpu.VMEM)[0]
    grad_small = jnp.sum(small_every, axis=0).reshape(-1)[: small_terms.shape[1]]
    masters = (w_qkv, w_out, w_gate_up, w_down, small_params)
    grads = (grad_qkv, grad_out, grad_gate_up, grad_down, grad_small)
    firsts = (first_qkv, first_out, first_gate_up, first_down, first_small)
    seconds = (second_qkv, second_out, second_gate_up, second_down, second_small)
    small_offset = place_of(EVERY) * small_params.shape[0]
    labels = (
        part_labels(QKV, [heads_width, heads_width + kv_width], 0, 0),
        part_labels(D, [], 3, 0),
        part_labels(2 * FF, [FF], 4, 0),
        part_labels(D, [], 6, 0),
        part_labels(
            small_params.shape[0],
            [heads_width, heads_width + kv_width, QKV, QKV + D],
            7,
            small_offset,
        ),
    )
    grad_local = jnp.sum(jnp.stack([jnp.sum(grad * grad) for grad in grads]))
    weight_local = jnp.sum(
        jnp.stack(
            [piece_sums(column_squares(master), label) for master, label in zip(masters, labels)]
        ),
        axis=0,
    )
    totals = jnp.sum(tiny_gather(jnp.concatenate([weight_local, grad_local[None]]), 7), axis=0)
    weight_total, grad_total = totals[:piece_count], totals[piece_count]
    grad_norm = jnp.sqrt(grad_total)
    factor = jnp.minimum(1.0, math.sqrt(NPARAMS) / grad_norm)
    results = []
    for master, grad, first, second in zip(masters, grads, firsts, seconds):
        clipped = grad * factor
        first_new = beta_one * first + (1.0 - beta_one) * clipped
        second_new = beta_two * second + (1.0 - beta_two) * clipped * clipped
        update = (
            first_new
            / (1.0 - beta_one**step_count)
            / (jnp.sqrt(second_new / (1.0 - beta_two**step_count)) + lamb_eps)
            + decay_rate * master
        )
        results.append((first_new, second_new, update))
    update_local = jnp.sum(
        jnp.stack(
            [piece_sums(column_squares(item[2]), label) for item, label in zip(results, labels)]
        ),
        axis=0,
    )
    update_total = jnp.sum(tiny_gather(update_local, 8), axis=0)
    weight_norm = jnp.sqrt(weight_total)
    update_norm = jnp.sqrt(update_total)
    trust = weight_norm / (update_norm + trust_eps)
    updated = [
        master - learn_rate * spread_trust(trust, label) * item[2]
        for master, item, label in zip(masters, results, labels)
    ]
    matrix_norms = jnp.stack([weight_norm, update_norm])
    return (
        block_out,
        tokens_grad,
        grad_norm,
        matrix_norms,
        updated[0],
        updated[1],
        updated[2],
        updated[3],
        updated[4],
        results[0][0],
        results[1][0],
        results[2][0],
        results[3][0],
        results[4][0],
        results[0][1],
        results[1][1],
        results[2][1],
        results[3][1],
        results[4][1],
    )


def solution(mesh):
    seq, fsdp = mesh.shape["seq"], mesh.shape["fsdp"]
    deep = 4 if fsdp % 4 == 0 else 1
    mesh = Mesh(mesh.devices.reshape(seq // 2, 2, deep, fsdp // deep), EVERY)
    return jax.shard_map(
        shards,
        mesh=mesh,
        in_specs=(
            P(("z", "y"), ("x", "core"), None),
            P(("z", "y"), ("x", "core"), None),
            P(("z", "y"), None),
            P(EVERY, None),
            P(EVERY, None),
            P(EVERY, None),
            P(EVERY, None),
            P(EVERY),
            P(EVERY, None),
            P(EVERY, None),
            P(EVERY, None),
            P(EVERY, None),
            P(EVERY),
            P(EVERY, None),
            P(EVERY, None),
            P(EVERY, None),
            P(EVERY, None),
            P(EVERY),
        ),
        out_specs=(
            P(("z", "y"), ("x", "core"), None),
            P(("z", "y"), ("x", "core"), None),
            P(),
            P(),
            P(EVERY, None),
            P(EVERY, None),
            P(EVERY, None),
            P(EVERY, None),
            P(EVERY),
            P(EVERY, None),
            P(EVERY, None),
            P(EVERY, None),
            P(EVERY, None),
            P(EVERY),
            P(EVERY, None),
            P(EVERY, None),
            P(EVERY, None),
            P(EVERY, None),
            P(EVERY),
        ),
        check_vma=False,
    )
```
